32 devices in a mesh: wa: 2 (over x), pb: 4 (over y, core), ka: 4 (over z).
Axes of the slice: x: 2, y: 2, z: 4, core: 2. Of those that a mesh axis runs over, the one named last changes fastest.
Arguments:
- slater: bfloat16 [768, 9216], P(('wa', 'pb', 'ka')), may hold values from -6 to 6
- inverse: bfloat16 [768, 2304], P(('wa', 'pb', 'ka')), may hold values from -1.75 to 1.75
- send_rows: int32 [64, 3], P(('wa', 'pb', 'ka')), may hold values from 0 to 23
- take_rows: int32 [768], P(('wa', 'pb', 'ka')), may hold values from 0 to 29, as said below
- pair_table: int32 [4, 16], replicated, may hold values from 0 to 15, each once within a row
- rotated_chol: bfloat16 [4, 9216, 512], P('pb', 'ka'), may hold values from -0.0625 to 0.0625
- chol_vectors: bfloat16 [4, 512, 36864], P('pb', None, 'ka'), may hold values from -0.125 to 0.125
- aux_noise: bfloat16 [768, 2048], P('wa', 'pb'), may hold values from -6 to 6
Outputs:
- moved_walkers: bfloat16 [768, 9216], P(('wa', 'pb', 'ka'))
- fields: bfloat16 [768, 2048], P('wa', 'pb')
The draws below stay inside these ranges and needn't reach their ends.
Inputs may be any that keep to these rules, and one draw needn't show every extreme that they name: `pair_table`: each row of a momentum transfer is a permutation of the 16 k-points. `send_rows`: row b * 2 + d lists the local rows (0 to 23) of the walkers that the device of block b sends to the device with wa index d and the same pb and ka indices; only the first entries that the receiver takes are read. `take_rows`: A slot's value t below 24 names the device's own walker t; t = 24 + s * 3 + j names entry j of the list that the device with wa index s (same pb and ka indices) sends to this device. s is never the device's own wa index; from each source the entries used are its first ones, each used by one slot only, at most 3 of them; on every device some source fills all 3, and on some device every other source does.
All inputs are finite; a program needn't handle non-finite values.
Results may differ from the reference program's by a relative error of at most 0.015.
Values may be sent and summed in bfloat16 or wider, within the bound.
No kernel may reach another device: no remote copies, remote signals or barrier semaphores. Data moves between devices by JAX's collectives and lax.ppermute only.
A program may use at most 128 MiB of HBM per device.

```python
import math
import jax
import jax.numpy as jnp
from jax import lax

NK = 16
NORB = 48
NOCC = 12
NCHOL = 512
WB = 24
PAIR = 3
NQ = 4
WGROUPS = 2
BLOCKS = 32
WALKERS = 768


def draw_take_rows(key, part):
    blocks = WALKERS // WB
    groups = WGROUPS
    per_group = blocks // groups
    key_count, key_force, key_full, key_local, key_perm = jax.random.split(jax.random.fold_in(key, 7), 5)
    counts = jax.random.randint(key_count, (blocks, groups), 0, PAIR + 1)
    dest_group = jnp.arange(blocks) // per_group
    offset_group = jax.random.randint(key_force, (blocks,), 1, groups)
    forced = (dest_group + offset_group) % groups
    sources = jnp.arange(groups)
    counts = jnp.where(sources[None, :] == forced[:, None], PAIR, counts)
    full_block = jax.random.randint(key_full, (), 0, blocks - per_group)
    counts = jnp.where(jnp.arange(blocks)[:, None] == full_block, PAIR, counts)
    counts = jnp.where(sources[None, :] == dest_group[:, None], 0, counts)
    stop_at = jnp.cumsum(counts, axis=1)
    starts = stop_at - counts
    slot_ids = jnp.arange(WB)
    group_of = jnp.sum((stop_at[:, None, :] <= slot_ids[None, :, None]).astype(jnp.int32), axis=2)
    group_of = jnp.minimum(group_of, groups - 1)
    offset = slot_ids[None, :] - jnp.take_along_axis(starts, group_of, axis=1)
    remote = WB + group_of * PAIR + offset
    local_rows = jax.random.randint(key_local, (blocks, WB), 0, WB)
    values = jnp.where(slot_ids[None, :] < stop_at[:, -1:], remote, local_rows)
    block_keys = jax.random.split(key_perm, blocks)
    shuffles = jax.vmap(lambda one_key: jax.random.permutation(one_key, WB))(block_keys)
    return jnp.take_along_axis(values, shuffles, axis=1).reshape(-1).astype(jnp.int32)


def touch_ends(result, rng, smallest, high):
    place = [jax.random.randint(jax.random.fold_in(rng, axis), (), 0, length) for axis, length in enumerate(result.shape)]
    widest = result.shape.index(max(result.shape))
    next_to = place[:widest] + [(place[widest] + 1) % result.shape[widest]] + place[widest + 1:]
    return result.at[tuple(place)].set(smallest).at[tuple(next_to)].set(high)


def shard_levels(key, shape, cuts, least, top_value):
    def one(dim, parts):
        draws = jax.random.uniform(jax.random.fold_in(jax.random.fold_in(key, 6), dim), (parts,), jnp.float32, least / len(cuts), top_value / len(cuts))
        return jnp.repeat(jnp.exp(draws), shape[dim] // parts).reshape((-1,) + (1,) * (len(shape) - dim - 1))

    level = one(*cuts[0])
    for cut in cuts[1:]:
        level = level * one(*cut)
    return level


def noise(own_key, shape, scale, most, cuts=(), held_as=jnp.bfloat16):
    drawn = jax.random.normal(own_key, shape, jnp.float32) * scale
    if len(cuts) > 0:
        drawn = shard_levels(own_key, shape, cuts, -0.22, 0.18) * drawn
    return jnp.clip(drawn, min=-most, max=most).astype(held_as)


def setup_inputs(seed: int = 0) -> dict:
    streams_of = jax.random.split(jax.random.key(seed), 9)
    return {
        "slater": noise(streams_of[0], (WALKERS, NK * NORB * NOCC), 1.0, 6.0, ((0, 32),)),
        "inverse": noise(streams_of[1], (WALKERS, NK * NOCC * NOCC), NOCC ** -0.5, 1.75, ((0, 32),)),
        "send_rows": touch_ends(jax.random.randint(streams_of[2], (BLOCKS * WGROUPS, PAIR), 0, WB), jax.random.fold_in(streams_of[2], 1), 0, WB - 1).astype(jnp.int32),
        "take_rows": draw_take_rows(jax.random.fold_in(streams_of[8], 71), 0),
        "pair_table": jax.vmap(lambda own: jax.random.permutation(own, NK))(jax.random.split(streams_of[4], NQ)).reshape((NQ, NK)).astype(jnp.int32),
        "rotated_chol": noise(streams_of[5], (NQ, NK * NOCC * NORB, NCHOL), (NK * NOCC * NORB) ** -0.5, 0.0625, ((0, 4), (1, 4))),
        "chol_vectors": noise(streams_of[6], (NQ, NCHOL, NK * NORB * NORB), (NQ * NCHOL) ** -0.5, 0.125, ((0, 4), (2, 4))),
        "aux_noise": noise(streams_of[7], (WALKERS, NQ * NCHOL), 1.0, 6.0, ((0, 2), (1, 4))),
    }


tau_coef = 2.0
force_coef = 0.5

def propagate(potential, slater_mats):
    potential = lax.optimization_barrier(potential)
    matrix = potential.astype(jnp.float32)
    taylor_term = slater_mats.astype(jnp.float32)
    summed = taylor_term
    step_size = tau_coef / math.sqrt(NORB)
    for degree in range(1, 7):
        taylor_term = jnp.einsum('rkpq,rkqi->rkpi', matrix, taylor_term, precision=lax.Precision.HIGHEST) * (-step_size / degree)
        summed = summed + taylor_term
    return summed.astype(jnp.bfloat16)

def source_rows(send_rows, take_rows):
    groups = WGROUPS
    per_group = BLOCKS // groups
    walker_ids = jnp.arange(WALKERS, dtype=jnp.int32)
    block_index = walker_ids // WB
    dest_group = block_index // per_group
    column = block_index % per_group
    remote_slot = jnp.maximum(take_rows - WB, 0)
    source_group = jnp.minimum(remote_slot // PAIR, groups - 1)
    slot_index = remote_slot % PAIR
    source_block = source_group * per_group + column
    sent_rows = send_rows[source_block * groups + dest_group, slot_index]
    return jnp.where(take_rows < WB, block_index * WB + take_rows, source_block * WB + sent_rows).astype(jnp.int32)

def reference(slater, inverse, send_rows, take_rows, pair_table, rotated_chol, chol_vectors, aux_noise):
    sources = source_rows(send_rows, take_rows)
    walker_slater = jnp.take(slater, sources, axis=0)
    walker_inverse = jnp.take(inverse, sources, axis=0)
    inverse_mats = walker_inverse.reshape(WALKERS, NK, NOCC, NOCC).astype(jnp.float32)
    slater_mats = walker_slater.reshape(WALKERS, NK, NORB, NOCC).astype(jnp.float32)
    greens = jnp.einsum('wkij,wkrj->wkir', inverse_mats, slater_mats, precision=lax.Precision.HIGHEST)
    greens = greens.astype(jnp.bfloat16).reshape(WALKERS, NK, NOCC * NORB)
    force_parts = []
    for momentum in range(NQ):
        picked = jnp.take(greens, pair_table[momentum], axis=1).reshape(WALKERS, NK * NOCC * NORB)
        force_parts.append(jnp.dot(picked, rotated_chol[momentum], preferred_element_type=jnp.float32))
    force_bias = jnp.concatenate(force_parts, axis=1)
    fields = (aux_noise.astype(jnp.float32) - force_coef * force_bias).astype(jnp.bfloat16)

    def one_block(block_pair):
        block_fields, block_slater = block_pair
        summed = jnp.zeros((WB, NK * NORB * NORB), jnp.float32)
        for momentum in range(NQ):
            term_piece = jnp.dot(block_fields[:, momentum * NCHOL:(momentum + 1) * NCHOL], chol_vectors[momentum], preferred_element_type=jnp.float32).astype(jnp.bfloat16)
            term_piece = lax.optimization_barrier(term_piece)
            summed = summed + term_piece.astype(jnp.float32)
        potential = summed.astype(jnp.bfloat16).reshape(WB, NK, NORB, NORB)
        return propagate(potential, block_slater.reshape(WB, NK, NORB, NOCC)).reshape(WB, NK * NORB * NOCC)
    propagated = lax.map(one_block, (fields.reshape(BLOCKS, WB, NQ * NCHOL), walker_slater.reshape(BLOCKS, WB, NK * NORB * NOCC)))
    return (propagated.reshape(WALKERS, NK * NORB * NOCC), fields)
```

```python
import functools
import math

import jax
import jax.numpy as jnp
from jax import lax
from jax.experimental import pallas as pl
from jax.experimental.pallas import tpu as pltpu
from jax.sharding import PartitionSpec as P

tau_coef = 2.0
force_coef = 0.5
DEGREES = 6

BF = jnp.bfloat16
F32 = jnp.float32
VMEM = pl.BlockSpec(memory_space=pltpu.VMEM)
SMEM = pl.BlockSpec(memory_space=pltpu.SMEM)
LANES = 128


def call(kernel, out, n_smem, n_vmem, scratch=(), flops=0, bytes_accessed=0):
    return pl.pallas_call(
        kernel,
        out_shape=out,
        in_specs=[SMEM] * n_smem + [VMEM] * n_vmem,
        out_specs=jax.tree.map(lambda _: VMEM, out),
        scratch_shapes=list(scratch),
        cost_estimate=pl.CostEstimate(
            flops=flops, bytes_accessed=bytes_accessed, transcendentals=0
        ),
    )


def one_hot(picks, rows, depth):
    row = lax.broadcasted_iota(jnp.int32, (rows, depth), 0)
    column = lax.broadcasted_iota(jnp.int32, (rows, depth), 1)
    target = jnp.full((rows, depth), -1, jnp.int32)
    for r, pick in enumerate(picks):
        target = jnp.where(row == r, pick, target)
    return jnp.where(target == column, 1.0, 0.0).astype(BF)


def at_columns(index, count, width, action):
    if width % LANES == 0:
        action(pl.multiple_of(index * width, width))
        return
    for i in range(count):
        pl.when(index == i)(functools.partial(action, i * width))


def send_kernel(groups, pair, where_ref, send_ref, slater_ref, inverse_ref, out_ref):
    me = where_ref[0]
    picks = []
    for shift in range(1, groups):
        to = lax.rem(me + shift, groups)
        picks += [send_ref[to, j] for j in range(pair)]
    select = one_hot(picks, len(picks), slater_ref.shape[0])
    wide = slater_ref.shape[1]
    got = jnp.dot(select, slater_ref[...], preferred_element_type=F32).astype(BF)
    out_ref[:, pl.ds(0, wide)] = got
    got = jnp.dot(select, inverse_ref[...], preferred_element_type=F32).astype(BF)
    out_ref[:, pl.ds(wide, inverse_ref.shape[1])] = got


def up(n, to):
    return -(-n // to) * to


def green_kernel(
    groups, pair, nk, norb, nocc, momenta, kgroups,
    where_ref, take_ref, table_ref, slater_ref, inverse_ref, got_ref, *rest,
):
    blocks = momenta * kgroups
    routed = rest[:blocks]
    outgoing = rest[blocks : blocks + 2 * kgroups]
    sel, inv, turned, spread, inv_t, greens_t, greens = rest[blocks + 2 * kgroups :]
    wb = slater_ref.shape[0]
    wide, narrow = slater_ref.shape[1], inverse_ref.shape[1]
    me_wa, me_pb, me_ka = where_ref[0], where_ref[1], where_ref[2]
    one_k, one_inv = norb * nocc, nocc * nocc
    local_k = nk // kgroups

    picks_own, picks_got = [], []
    for w in range(wb):
        t = take_ref[w]
        rest_t = jnp.maximum(t - wb, 0)
        s = lax.div(rest_t, pair)
        j = lax.rem(rest_t, pair)
        shift = lax.rem(me_wa - s + groups, groups)
        picks_own.append(jnp.where(t < wb, t, -2))
        picks_got.append(jnp.where(t < wb, -2, (shift - 1) * pair + j))
    own = one_hot(picks_own, wb, wb)
    got = one_hot(picks_got, wb, got_ref.shape[0])
    sel[...] = jnp.dot(own, slater_ref[...], preferred_element_type=F32) + jnp.dot(
        got, got_ref[:, pl.ds(0, wide)], preferred_element_type=F32
    )
    inv[...] = jnp.dot(own, inverse_ref[...], preferred_element_type=F32) + jnp.dot(
        got, got_ref[:, pl.ds(wide, narrow)], preferred_element_type=F32
    )

    half_wide = local_k // 2 * one_k
    for d in range(kgroups):
        for b in range(2):
            at = jnp.bitwise_xor(me_ka, d) * 2 + jnp.bitwise_xor(lax.rem(me_pb, 2), b)

            def take(chosen, to=outgoing[d * 2 + b]):
                to[...] = sel[:, pl.ds(chosen, half_wide)].astype(BF)

            at_columns(at, 2 * kgroups, half_wide, take)

    pairs = nk // 2
    lanes = up(pairs * wb, LANES)
    pad = lanes - pairs * wb
    rows = [sel[:, p * 2 * one_k : (p + 1) * 2 * one_k] for p in range(pairs)]
    rows.append(jnp.zeros((pad, 2 * one_k), F32))
    block = jnp.concatenate(rows, axis=0)
    tiles = lanes // LANES
    for t in range(tiles):
        turned[t] = block[t * LANES : (t + 1) * LANES].T
    for kk in range(2):
        rows = [
            inv[:, (2 * p + kk) * one_inv : (2 * p + kk + 1) * one_inv]
            for p in range(pairs)
        ]
        rows.append(jnp.zeros((pad, one_inv), F32))
        block = jnp.concatenate(rows, axis=0)
        block = jnp.concatenate(
            [block, jnp.zeros((lanes, up(one_inv, LANES) - one_inv), F32)], axis=1
        )
        back = []
        for t in range(tiles):
            inv_t[...] = block[t * LANES : (t + 1) * LANES].T
            for j in range(nocc):
                spread[pl.ds(j * norb, norb), :] = turned[
                    t, pl.ds(kk * one_k + j, norb, stride=nocc), :
                ]

            def one_row(i, carry):
                total = jnp.zeros((norb, LANES), F32)
                for j in range(nocc):
                    total = total + spread[pl.ds(j * norb, norb), :] * inv_t[
                        pl.ds(i * nocc + j, 1), :
                    ]
                greens_t[pl.ds(pl.multiple_of(i * norb, norb), norb), :] = total
                return carry

            lax.fori_loop(0, nocc, one_row, 0)
            back.append(greens_t[...].T)
        back = jnp.concatenate(back, axis=0)
        for p in range(pairs):
            greens[2 * p + kk] = back[p * wb : (p + 1) * wb, :one_k]
    for p in range(blocks):
        q = jnp.bitwise_xor(me_pb, p // kgroups)
        c = jnp.bitwise_xor(me_ka, p % kgroups)
        parts = [greens[table_ref[q, c * local_k + l]] for l in range(local_k)]
        routed[p][...] = jnp.concatenate(parts, axis=1).astype(BF)


def force_kernel(n, *refs):
    parts = jnp.concatenate([r[...].astype(F32) for r in refs[:n]], axis=0).astype(BF)
    chol_ref, out_ref = refs[n], refs[n + 1]
    out_ref[...] = jnp.dot(parts, chol_ref[0], preferred_element_type=F32).astype(BF)


def field_kernel(momenta, kgroups, where_ref, noise_ref, *refs):
    out_ref = refs[kgroups]
    me_pb, me_ka = where_ref[1], where_ref[2]
    total = refs[0][...].astype(F32)
    for d in range(1, kgroups):
        total = total + refs[d][...].astype(F32)
    rows = [
        noise_ref[jnp.bitwise_xor(me_pb, p) * kgroups + me_ka].astype(F32)
        for p in range(momenta)
    ]
    out_ref[...] = (jnp.concatenate(rows, axis=0) - force_coef * total).astype(BF)


def potential_kernel(wb, where_ref, f_ref, g_ref, own_ref, other_ref, keep_ref, send_ref):
    g = g_ref[...].astype(F32)
    pieces = [g[p * wb : (p + 1) * wb] for p in range(g.shape[0] // wb)]
    swapped = [pieces[p ^ 1] for p in range(len(pieces))]
    g = jnp.concatenate(swapped, axis=0).astype(BF)
    total = jnp.dot(f_ref[...], own_ref[0], preferred_element_type=F32)
    total = total + jnp.dot(g, other_ref[...], preferred_element_type=F32)
    half = total.shape[0] // 2
    keep_ref[...] = total[:half].astype(BF)
    send_ref[...] = total[half:].astype(BF)


def potential_call(where, f, g, own, other, wb):
    rows, depth = f.shape
    columns = other.shape[1]
    steps = 4 if columns % (4 * LANES) == 0 else 1
    tile = columns // steps
    spec = pltpu.PrefetchScalarGridSpec(
        num_scalar_prefetch=1,
        grid=(steps,),
        in_specs=[
            pl.BlockSpec((rows, depth), lambda s, w: (0, 0)),
            pl.BlockSpec((rows, depth), lambda s, w: (0, 0)),
            pl.BlockSpec((1, depth, tile), lambda s, w: (0, 0, lax.rem(w[1], 2) * steps + s)),
            pl.BlockSpec((depth, tile), lambda s, w: (0, s)),
        ],
        out_specs=[
            pl.BlockSpec((rows // 2, tile), lambda s, w: (0, s)),
            pl.BlockSpec((rows // 2, tile), lambda s, w: (0, s)),
        ],
    )
    out = jax.ShapeDtypeStruct((rows // 2, columns), BF)
    return pl.pallas_call(
        functools.partial(potential_kernel, wb),
        grid_spec=spec,
        out_shape=[out, out],
        cost_estimate=pl.CostEstimate(
            flops=4 * rows * depth * columns,
            bytes_accessed=4 * depth * columns,
            transcendentals=0,
        ),
    )(where, f, g, own, other)


def taylor_kernel(norb, nocc, keep_ref, got_ref, s0_ref, s1_ref, out0, out1, vt, v, xt, x, sums):
    one_k = norb * nocc
    wb = s0_ref.shape[0]
    halves = keep_ref.shape[1] // (norb * norb)
    used = halves * 2 * wb
    lanes = LANES
    pot = keep_ref[...].astype(F32) + got_ref[...].astype(F32)
    pot = pot * (-tau_coef / math.sqrt(norb))
    rows = [pot[:, h * norb * norb : (h + 1) * norb * norb] for h in range(halves)]
    rows.append(jnp.zeros((lanes - used, norb * norb), F32))
    vt[...] = jnp.concatenate(rows, axis=0).T
    for q in range(norb):
        v[pl.ds(q * norb, norb), :] = vt[pl.ds(q, norb, stride=norb), :]
    rows = []
    for h in range(halves):
        for s in (s0_ref, s1_ref):
            rows.append(s[...].astype(F32)[:, h * one_k : (h + 1) * one_k])
    rows.append(jnp.zeros((lanes - used, one_k), F32))
    block = jnp.concatenate(rows, axis=0)
    block = jnp.concatenate(
        [block, jnp.zeros((lanes, up(one_k, LANES) - one_k), F32)], axis=1
    )
    xt[...] = block.T
    for i in range(nocc):
        start = xt[pl.ds(i, norb, stride=nocc), :]
        x[0, pl.ds(i * norb, norb), :] = start
        sums[pl.ds(i * norb, norb), :] = start
    step = 4
    blocks = nocc // step

    def one(n, carry):
        m = n // blocks
        i0 = (n - m * blocks) * step
        now = lax.rem(m, 2)
        scale = 1.0 / (m + 1).astype(F32)
        acc = [jnp.zeros((norb, lanes), F32) for _ in range(step)]
        for q in range(norb):
            column = v[pl.ds(q * norb, norb), :]
            for a in range(step):
                acc[a] = acc[a] + column * x[now, pl.ds((i0 + a) * norb + q, 1), :]
        for a in range(step):
            at = pl.ds(pl.multiple_of((i0 + a) * norb, norb), norb)
            term = acc[a] * scale
            x[1 - now, at, :] = term
            sums[at, :] = sums[at, :] + term
        return carry

    lax.fori_loop(0, DEGREES * blocks, one, 0)
    for i in range(nocc):
        xt[pl.ds(i, norb, stride=nocc), :] = sums[pl.ds(i * norb, norb), :]
    back = xt[...].T
    for b, out in enumerate((out0, out1)):
        parts = []
        for h in range(halves):
            at = (h * 2 + b) * wb
            parts.append(back[at : at + wb, :one_k])
        out[...] = jnp.concatenate(parts, axis=1).astype(BF)


def gather_kernel(kgroups, where_ref, *refs):
    out_ref = refs[2 * kgroups]
    me_pb, me_ka = where_ref[1], where_ref[2]
    wide = refs[0].shape[1]
    for d in range(kgroups):
        for b in range(2):
            at = jnp.bitwise_xor(me_ka, d) * 2 + jnp.bitwise_xor(lax.rem(me_pb, 2), b)

            def put(chosen, ref=refs[d * 2 + b]):
                out_ref[:, pl.ds(chosen, wide)] = ref[...]

            at_columns(at, 2 * kgroups, wide, put)


def fields_kernel(momenta, kgroups, where_ref, *refs):
    out_ref = refs[kgroups]
    me_pb, me_ka = where_ref[1], where_ref[2]
    wb = out_ref.shape[1]
    for d in range(kgroups):
        piece = refs[d][...].astype(F32)
        for p in range(momenta):
            at = jnp.bitwise_xor(me_pb, p) * kgroups + jnp.bitwise_xor(me_ka, d)
            out_ref[at] = piece[p * wb : (p + 1) * wb].astype(BF)


def body(slater, inverse, send_rows, take_rows, pair_table, rotated_chol, chol_vectors, aux_noise):
    groups = lax.axis_size("wa")
    momenta = lax.axis_size("pb")
    kgroups = lax.axis_size("ka")
    wb = slater.shape[0]
    pair = send_rows.shape[1]
    nk = pair_table.shape[1]
    nocc = math.isqrt(inverse.shape[1] // nk)
    norb = slater.shape[1] // (nk * nocc)
    nchol = rotated_chol.shape[2]
    one_k = norb * nocc
    local_k = nk // kgroups
    blocks = momenta * kgroups
    wide, narrow = slater.shape[1], inverse.shape[1]
    where = jnp.stack(
        [lax.axis_index("wa"), lax.axis_index("pb"), lax.axis_index("ka")]
    ).astype(jnp.int32)
    lo = lax.rem(lax.axis_index("pb"), 2)

    def hop(value, p, d):
        if p == 0 and d == 0:
            return value
        flip = p * kgroups + d
        return lax.ppermute(value, ("pb", "ka"), [(i, i ^ flip) for i in range(blocks)])

    sent = call(
        functools.partial(send_kernel, groups, pair),
        jax.ShapeDtypeStruct(((groups - 1) * pair, wide + narrow), BF), 2, 2,
    )(where, send_rows, slater, inverse)
    got = [
        lax.ppermute(
            sent[(shift - 1) * pair : shift * pair], "wa",
            [(i, (i + shift) % groups) for i in range(groups)],
        )
        for shift in range(1, groups)
    ]
    got = got[0] if len(got) == 1 else jnp.concatenate(got, axis=0)

    columns = chol_vectors.shape[2] // 2
    give = lax.dynamic_slice(
        chol_vectors, (0, 0, (1 - lo) * columns), (1, nchol, columns)
    )[0]
    chol_other = hop(give, 1, 0)

    pairs = nk // 2
    lanes = up(pairs * wb, LANES)
    outs = call(
        functools.partial(green_kernel, groups, pair, nk, norb, nocc, momenta, kgroups),
        [jax.ShapeDtypeStruct((wb, local_k * one_k), BF)] * blocks
        + [jax.ShapeDtypeStruct((wb, local_k // 2 * one_k), BF)] * (2 * kgroups),
        3, 3,
        scratch=[
            pltpu.VMEM((wb, wide), F32),
            pltpu.VMEM((wb, narrow), F32),
            pltpu.VMEM((lanes // LANES, 2 * one_k, LANES), F32),
            pltpu.VMEM((one_k, LANES), F32),
            pltpu.VMEM((up(nocc * nocc, LANES), LANES), F32),
            pltpu.VMEM((up(one_k, LANES), LANES), F32),
            pltpu.VMEM((nk, wb, one_k), F32),
        ],
    )(where, take_rows, pair_table, slater, inverse, got)
    routed, outgoing = outs[:blocks], outs[blocks:]

    partial = []
    for d in range(kgroups):
        arrived = [hop(routed[p * kgroups + d], p, d) for p in range(momenta)]
        partial.append(
            call(
                functools.partial(force_kernel, momenta),
                jax.ShapeDtypeStruct((momenta * wb, nchol), BF), 0, momenta + 1,
                flops=2 * momenta * wb * local_k * one_k * nchol,
                bytes_accessed=2 * local_k * one_k * nchol,
            )(*arrived, rotated_chol)
        )
    shares = [partial[0]] + [hop(partial[d], 0, d) for d in range(1, kgroups)]
    own_fields = call(
        functools.partial(field_kernel, momenta, kgroups),
        jax.ShapeDtypeStruct((momenta * wb, nchol), BF), 1, 1 + kgroups,
    )(where, aux_noise.reshape(blocks, wb, nchol), *shares)
    pieces = [hop(own_fields, 0, d) for d in range(kgroups)]
    fields = call(
        functools.partial(fields_kernel, momenta, kgroups),
        jax.ShapeDtypeStruct((blocks, wb, nchol), BF), 1, kgroups,
    )(where, *pieces).reshape(blocks * wb, nchol)

    moved = [None] * (2 * kgroups)
    for d in range(kgroups):
        keep, send = potential_call(
            where, pieces[d], hop(pieces[d], 1, 0), chol_vectors, chol_other, wb
        )
        other = hop(send, 2, 0)
        mine = [hop(outgoing[d * 2 + b], b, d) for b in range(2)]
        out = jax.ShapeDtypeStruct((wb, local_k // 2 * one_k), BF)
        done = call(
            functools.partial(taylor_kernel, norb, nocc), [out, out], 0, 4,
            scratch=[
                pltpu.VMEM((norb * norb, LANES), F32),
                pltpu.VMEM((norb * norb, LANES), F32),
                pltpu.VMEM((up(one_k, LANES), LANES), F32),
                pltpu.VMEM((2, one_k, LANES), F32),
                pltpu.VMEM((one_k, LANES), F32),
            ],
            flops=10**9, bytes_accessed=10**6,
        )(keep, other, *mine)
        for b in range(2):
            moved[d * 2 + b] = hop(done[b], b, d)
    result = call(
        functools.partial(gather_kernel, kgroups),
        jax.ShapeDtypeStruct((wb, wide), BF), 1, 2 * kgroups,
    )(where, *moved)
    return result, fields


def solution(mesh):
    placed = (
        P(("wa", "pb", "ka"), None),
        P(("wa", "pb", "ka"), None),
        P(("wa", "pb", "ka"), None),
        P(("wa", "pb", "ka")),
        P(),
        P("pb", "ka", None),
        P("pb", None, "ka"),
        P("wa", "pb"),
    )
    return jax.shard_map(
        body,
        mesh=mesh,
        in_specs=placed,
        out_specs=(P(("wa", "pb", "ka"), None), P("wa", "pb")),
        check_vma=False,
    )
```
